256 devices in a mesh: grp: 64 (over z, y_hi, x), rep: 4 (over y_lo, core).
Axes of the slice: x: 4, y: 4 (y_hi: 2, y_lo: 2; y = y_hi * 2 + y_lo), z: 8, core: 2. Of those that a mesh axis runs over, the one named last changes fastest.
Arguments:
- embeddings: bfloat16 [65536, 1024], P(('grp', 'rep')), may hold values from -15 to 15
- scales: float32 [65536, 8], P(('grp', 'rep')), may hold values from 0.05 to 0.5
- cluster: int32 [65536], P(('grp', 'rep')), may hold values from 0 to 767, as said below
- cluster_rank: int32 [65536], P(('grp', 'rep')), may hold values from 0 to 63, as said below
Outputs:
- best_cosine: float32 [65536], P(('grp', 'rep'))
The draws below stay inside these ranges and needn't reach their ends.
Inputs may be any that keep to these rules, and one draw needn't show every extreme that they name: cluster // 12 names the owner of a row's cluster among 64 and cluster % 12 its place there; clusters of different shards are different even with equal numbers. Among the rows of one device at most 12 have the same owner, and in every draw some owner is named by exactly 12 rows of every device of its shard. `cluster_rank`: within one cluster the ranks of its rows are 0 to its size minus 1, each once; a cluster holds at most 64 rows, and in every draw some cluster holds exactly 64.
All inputs are finite; a program needn't handle non-finite values.
Results may differ from the reference program's by a relative error of at most 0.00035.
The reference program's roundings to bfloat16 on the way (of `values`, `inverse_root` and `whitened`) count: a program that leaves them out, or rounds other values in their place, can miss the bound.
Values may be sent and summed in bfloat16 or wider, within the bound.
A program may use at most 64 MiB of HBM per device.

```python
import math
import jax
import jax.numpy as jnp
from jax import lax

D = 1024
BLK = 128
ROWS_DEV = 256
CMAX = 64
STEPS = 5
SLOT = 12
CPO = 12
CLUSTERS = 768
ROWS_ALL = 65536
N_GRP = 64
N_REP = 4


def shard_layout(shard_key):
    order_key, count_key, source_key, cell_key = jax.random.split(shard_key, 4)
    owner_rank = jax.random.permutation(order_key, N_GRP).astype(jnp.int32)
    remaining = ROWS_DEV - SLOT
    base_count = remaining // (N_GRP - 1)
    leftover = remaining - base_count * (N_GRP - 1)
    half_base = base_count // 2
    pair_total = (N_GRP - 1) // 2

    def source_counts(one_key):
        perm_key, swap_key = jax.random.split(one_key)
        ranking = jax.random.permutation(perm_key, N_GRP - 1)
        counts = base_count + (ranking < leftover).astype(jnp.int32)
        swap_size = jax.random.randint(swap_key, (pair_total,), -half_base, half_base + 1).astype(jnp.int32)
        change = jnp.zeros((N_GRP - 1,), jnp.int32)
        change = change.at[0:2 * pair_total:2].add(swap_size).at[1:2 * pair_total:2].add(-swap_size)
        return jnp.concatenate([jnp.full((1,), SLOT, jnp.int32), counts + change])
    by_rank = jax.vmap(source_counts)(jax.random.split(count_key, N_GRP))
    by_owner = by_rank[:, owner_rank]
    seg_ends = jnp.cumsum(by_owner, axis=1)
    seg_starts = seg_ends - by_owner

    def source_rows(one_key, src_ends, src_starts):
        position = jax.random.permutation(one_key, ROWS_DEV).astype(jnp.int32)
        owner_of = jnp.sum((src_ends[None, :] <= position[:, None]).astype(jnp.int32), axis=1)
        return (owner_of, position - src_starts[owner_of])
    owner_of, within = jax.vmap(source_rows)(jax.random.split(source_key, N_GRP), seg_ends, seg_starts)
    cell_total = N_GRP * SLOT

    def owner_cells(one_key, counts_in):
        shuffle = jax.random.permutation(one_key, cell_total).astype(jnp.int32)
        filled = (jnp.arange(SLOT)[None, :] < counts_in[:, None]).reshape(cell_total).astype(jnp.int32)
        occupied = jnp.zeros((cell_total,), jnp.int32).at[shuffle].set(filled)
        cell_grid = occupied.reshape(CPO, CMAX)
        earlier = jnp.cumsum(cell_grid, axis=1) - cell_grid
        return (shuffle, earlier.reshape(cell_total))
    shuffle, earlier = jax.vmap(owner_cells)(jax.random.split(cell_key, N_GRP), by_owner.T)
    source = jnp.arange(N_GRP, dtype=jnp.int32)[:, None]
    slot_pos = source * SLOT + within
    cell_of = shuffle[owner_of, slot_pos]
    cluster = owner_of * CPO + cell_of // CMAX
    rank_of = earlier[owner_of, cell_of]
    return (cluster, rank_of)


def layout(key):
    base_key = jax.random.fold_in(key, 4711)
    cluster, rank_of = jax.vmap(shard_layout)(jax.random.split(base_key, N_REP))
    cluster = jnp.transpose(cluster, (1, 0, 2)).reshape(ROWS_ALL).astype(jnp.int32)
    rank_of = jnp.transpose(rank_of, (1, 0, 2)).reshape(ROWS_ALL).astype(jnp.int32)
    return (cluster, rank_of)


def draw_cluster(key, part):
    return layout(key)[0]


def draw_cluster_rank(key, part):
    return layout(key)[1]


def draw_embeddings(key, part):
    cluster = layout(key)[0]
    base_key = jax.random.fold_in(key, 9127)
    key_list = jax.random.split(base_key, 6)
    row_ids = jnp.arange(ROWS_ALL)
    device_block = row_ids // ROWS_DEV
    shard_of = device_block % N_REP
    centroid = jax.random.normal(key_list[0], (N_REP * CLUSTERS, D), jnp.float32)
    picked = centroid[shard_of * CLUSTERS + cluster]
    jitter = jax.random.normal(key_list[1], (ROWS_ALL, D), jnp.float32)
    spread = jnp.exp(jax.random.uniform(key_list[2], (D,), jnp.float32, jnp.log(0.2), jnp.log(2.0)))
    block_total = ROWS_ALL // ROWS_DEV
    device_lean = jax.random.normal(key_list[3], (block_total, D), jnp.float32) * (12.0 / jnp.sqrt(D * 1.0))
    row_tilt = jax.random.normal(key_list[4], (ROWS_ALL, 1), jnp.float32)
    offset = 0.8 * jax.random.normal(key_list[5], (D,), jnp.float32)
    rising = 1.0 + 2.0 * device_block.astype(jnp.float32) / (block_total - 1)
    values = rising[:, None] * (spread[None, :] * (jitter + 1.2 * picked) + offset[None, :] + row_tilt * device_lean[device_block])
    return jnp.clip(0.4 * values, -15.0, 15.0).astype(jnp.bfloat16)


def level_of(rng, shape, cuts, low, largest):
    level = 1.0
    for dim, blocks in cuts:
        draws = jax.random.uniform(jax.random.fold_in(jax.random.fold_in(rng, 6), dim), (blocks,), jnp.float32, low / len(cuts), largest / len(cuts))
        level = level * jnp.repeat(jnp.exp(draws), shape[dim] // blocks).reshape((-1,) + (1,) * (len(shape) - 1 - dim))
    return level


def setup_inputs(seed: int = 0) -> dict:
    keys = jax.random.split(jax.random.key(seed), 5)
    return {
        "embeddings": draw_embeddings(jax.random.fold_in(keys[4], 71), 0),
        "scales": jnp.clip(jnp.exp(math.log(0.5) - 2.3025851 * jax.random.uniform(keys[1], (ROWS_ALL, D // BLK), jnp.float32) ** level_of(keys[1], (ROWS_ALL, D // BLK), ((0, 256),), -0.2, 0.2)), 0.05, 0.5),
        "cluster": draw_cluster(jax.random.fold_in(keys[4], 71), 0),
        "cluster_rank": draw_cluster_rank(jax.random.fold_in(keys[4], 71), 0),
    }


COV_EPS = 0.001
UNIT_EPS = 1e-06
EXACT_MODE = lax.Precision.HIGHEST

def whiten(values, inverse_root, average):
    offset = jnp.dot(average[None, :], inverse_root.astype(jnp.float32), precision=EXACT_MODE)
    projected = jnp.dot(values, inverse_root, preferred_element_type=jnp.float32) - offset
    energy = lax.optimization_barrier(jnp.sum(projected * projected, axis=1, keepdims=True))
    return (projected * lax.rsqrt(energy + UNIT_EPS)).astype(jnp.bfloat16)

def best_within(table, occupied, cluster_count):
    feat_dim = table.shape[1]
    tile_rows = table.astype(jnp.float32).reshape(cluster_count, CMAX, feat_dim)
    similar = jnp.einsum('cmd,cnd->cmn', tile_rows, tile_rows, precision=EXACT_MODE)
    present = occupied.reshape(cluster_count, CMAX)
    distinct = lax.broadcasted_iota(jnp.int32, (1, CMAX, CMAX), 1) != lax.broadcasted_iota(jnp.int32, (1, CMAX, CMAX), 2)
    allowed = present[:, :, None] & present[:, None, :] & distinct
    highest = lax.optimization_barrier(jnp.max(jnp.where(allowed, similar, -jnp.inf), axis=2))
    return jnp.maximum(highest, -1.0).reshape(cluster_count * CMAX)

def reference(embeddings, scales, cluster, cluster_rank):
    row_total, feat_dim = embeddings.shape
    num_blocks = scales.shape[1]
    grouped = embeddings.astype(jnp.float32).reshape(row_total, num_blocks, feat_dim // num_blocks) * scales[:, :, None]
    values = grouped.reshape(row_total, feat_dim).astype(jnp.bfloat16)
    gram_sum = lax.dot_general(values, values, (((0,), (0,)), ((), ())), preferred_element_type=jnp.float32)
    column_total = lax.optimization_barrier(jnp.sum(values, axis=0, dtype=jnp.float32))
    average = column_total / row_total
    identity = jnp.eye(feat_dim, dtype=jnp.float32)
    centred = gram_sum / row_total - average[:, None] * average[None, :] + COV_EPS * identity
    normed = centred / jnp.sqrt(jnp.sum(centred * centred))
    current = identity
    for repeat in range(STEPS):
        product = jnp.dot(normed, current, precision=EXACT_MODE)
        product = jnp.dot(product, current, precision=EXACT_MODE)
        product = jnp.dot(product, current, precision=EXACT_MODE)
        current = 1.5 * current - 0.5 * product
    inverse_root = current.astype(jnp.bfloat16)
    whitened = whiten(values, inverse_root, average)
    per_device = row_total // (N_GRP * N_REP)
    shard_units = whitened.reshape(N_GRP, N_REP, per_device, feat_dim).transpose(1, 0, 2, 3).reshape(N_REP, N_GRP * per_device, feat_dim)
    cell_all = (cluster * CMAX + cluster_rank).astype(jnp.int32)
    shard_cells = cell_all.reshape(N_GRP, N_REP, per_device).transpose(1, 0, 2).reshape(N_REP, N_GRP * per_device)
    cell_count = CLUSTERS * CMAX

    def one_shard(pair_in):
        unit_rows, cell_index = pair_in
        table = jnp.zeros((cell_count, feat_dim), jnp.bfloat16).at[cell_index].set(unit_rows)
        occupied = jnp.zeros((cell_count,), jnp.int32).at[cell_index].set(1) > 0
        return best_within(table, occupied, CLUSTERS)[cell_index]
    result = lax.map(one_shard, (shard_units, shard_cells))
    return result.reshape(N_REP, N_GRP, per_device).transpose(1, 0, 2).reshape(row_total)
```

```python
import jax
import jax.numpy as jnp
from jax import lax
from jax.experimental import pallas as pl
from jax.experimental.pallas import tpu as pltpu
from jax.sharding import PartitionSpec as P

MESH = pl.DeviceIdType.MESH
F32 = jnp.float32
BF16 = jnp.bfloat16

D = 1024
BLK = 128
ROWS = 256
ROW_TOTAL = 65536
NG = 64
CPO = 12
SLOT = 16
NROW = NG * SLOT
LABEL = 12
COV_EPS = 0.001
UNIT_EPS = 1e-06

SIZE = {"x": 4, "y": 4, "z": 8}
COLOURS = (("xyz", 1152), ("yzx", 768), ("zxy", 512))
HALF = sum(rows for _, rows in COLOURS)
BASES = (0, 1152, 1920)
SUMS = 36 * BLK
MB = 256
NB = D // MB


def block_row(i, j):
    return (i * 8 - (i * (i - 1)) // 2 + (j - i)) * BLK


def aligned(v, m=8):
    return pl.multiple_of(v, m)


def split(v):
    hi = v.astype(BF16)
    return hi, (v - hi.astype(F32)).astype(BF16)


def thirds(v):
    a = v.astype(BF16)
    rest = v - a.astype(F32)
    b = rest.astype(BF16)
    return a, b, (rest - b.astype(F32)).astype(BF16)


def inverse_sqrt(v):
    y = lax.rsqrt(v)
    y = y * (1.5 - 0.5 * (v * y) * y)
    return y * (1.5 - 0.5 * (v * y) * y)


def nn(a, b):
    return jnp.dot(a, b, preferred_element_type=F32)


def nt(a, b):
    return lax.dot_general(a, b, (((1,), (1,)), ((), ())), preferred_element_type=F32)


def tn(a, b):
    return lax.dot_general(a, b, (((0,), (0,)), ((), ())), preferred_element_type=F32)


def iota(shape, dim):
    return lax.broadcasted_iota(jnp.int32, shape, dim)


def kernel(emb, sca, clu, out, vals, tri, tot, buf0, buf1, buf2, buf3, disp, arr, ret, got,
           nh, nl, wh, mh, ml, ah, al, eh, qh, ql, zh, zl, th, tl, kh, kl, lin, acc, avg8, off,
           send_sem, recv_sem, a2a_send, a2a_recv):
    g = lax.axis_index("grp")
    r = lax.axis_index("rep")
    core = r % 2
    me = {"x": g % 4, "y": ((g // 4) % 2) * 2 + r // 2, "z": g // 8}

    def device(x, y, z, c):
        return (z * 8 + (y // 2) * 4 + x, (y % 2) * 2 + c)

    def peer(axis, d):
        at = dict(me)
        at[axis] = (me[axis] + d) % SIZE[axis]
        return device(at["x"], at["y"], at["z"], core)

    partner = (g, r + 1 - 2 * core)

    barrier = pltpu.get_barrier_semaphore()

    def greet(d, carry):
        pl.semaphore_signal(barrier, inc=1, device_id=((g + d) % NG, r), device_id_type=MESH)
        return carry

    lax.fori_loop(1, NG, greet, 0)
    for d in (1, 2, 3):
        pl.semaphore_signal(barrier, inc=1, device_id=peer("y", d), device_id_type=MESH)
    pl.semaphore_signal(barrier, inc=1, device_id=partner, device_id_type=MESH)

    for b in range(8):
        cols = slice(b * BLK, (b + 1) * BLK)
        v = (emb[:, cols].astype(F32) * sca[:, b:b + 1]).astype(BF16)
        vals[:, cols] = v
        tri[SUMS + b:SUMS + b + 1, :] = jnp.sum(v.astype(F32), axis=0, keepdims=True)
    tri[SUMS + 8:SUMS + 2 * BLK, :] = jnp.zeros((2 * BLK - 8, BLK), F32)
    for i in range(8):
        panel = tn(vals[:, i * BLK:(i + 1) * BLK], vals[:, i * BLK:])
        for j in range(i, 8):
            row = block_row(i, j)
            tri[row:row + BLK, :] = panel[:, (j - i) * BLK:(j - i + 1) * BLK]

    pl.semaphore_wait(barrier, NG - 1 + 3 + 1)

    sem_at = [0]

    def copies(todo):
        started = []
        for src, dst, to, slot in todo:
            desc = pltpu.make_async_remote_copy(
                src_ref=src, dst_ref=dst, send_sem=send_sem.at[slot], recv_sem=recv_sem.at[slot],
                device_id=to, device_id_type=MESH)
            desc.start()
            started.append(desc)
        return started

    every = []

    def launch(todo):
        started = copies(todo)
        every.extend(started)
        return started

    def fresh(n):
        first = sem_at[0]
        sem_at[0] += n
        return first

    mine = core * HALF
    other = HALF - mine
    pending = []
    for c, (axes, rows) in enumerate(COLOURS):
        s = fresh(1)
        pending.append(launch([(
            tri.at[pl.ds(aligned(other + BASES[c]), rows)], buf0.at[pl.ds(BASES[c], rows)], partner, s)]))

    cl_row = clu[...].astype(F32)
    cl_b = jnp.broadcast_to(cl_row, (ROWS, ROWS))
    cl_t = cl_b.T
    own_b = jnp.floor((cl_b + 0.5) * (1.0 / CPO))
    own_t = jnp.floor((cl_t + 0.5) * (1.0 / CPO))
    same = own_b == own_t
    si = iota((ROWS, ROWS), 0)
    li = iota((ROWS, ROWS), 1)
    slot_row = jnp.sum(jnp.where(same & (si < li), 1.0, 0.0), axis=0, keepdims=True)
    slot_col = jnp.sum(jnp.where(same & (li < si), 1.0, 0.0), axis=1, keepdims=True)
    own_row = own_b[0:1, :]
    label_at = slot_col * 16.0 + (cl_t[:, 0:1] - CPO * own_t[:, 0:1])
    labels = jnp.where(li.astype(F32) == label_at, 1.0, 0.0).astype(BF16)
    target = own_row * SLOT + slot_row
    label_row = own_row * SLOT + LABEL
    for k in range(4):
        rows = iota((256, ROWS), 0).astype(F32) + (k * 256.0)
        pick = jnp.where(rows == target, 1.0, 0.0).astype(BF16)
        pick_label = jnp.where(rows == label_row, 1.0, 0.0).astype(BF16)
        sorted_rows = nn(pick, vals[...])
        disp[k * 256:(k + 1) * 256, 256:] = sorted_rows[:, 256:].astype(BF16)
        disp[k * 256:(k + 1) * 256, 0:256] = (sorted_rows[:, 0:256] + nn(pick_label, labels)).astype(BF16)

    bases, sizes = [], []
    step1, step2, step3 = [], [], []
    for c, (axes, rows) in enumerate(COLOURS):
        for desc in pending[c]:
            desc.wait_recv()
        base = aligned(mine + BASES[c])
        tri[pl.ds(base, rows), :] += buf0[BASES[c]:BASES[c] + rows, :]
        n = SIZE[axes[0]]
        part = rows // n
        s = fresh(n - 1)
        step1.append(launch([(
            tri.at[pl.ds(aligned(base + ((me[axes[0]] + d) % n) * part), part)],
            buf1.at[pl.ds(BASES[c] + (n - 1 - d) * part, part)], peer(axes[0], d), s + n - 1 - d)
            for d in range(1, n)]))
    for c, (axes, rows) in enumerate(COLOURS):
        for desc in step1[c]:
            desc.wait_recv()
        n = SIZE[axes[0]]
        part = rows // n
        base = aligned(mine + BASES[c] + me[axes[0]] * part)
        total = tri[pl.ds(base, part), :]
        for k in range(n - 1):
            total = total + buf1[BASES[c] + k * part:BASES[c] + (k + 1) * part, :]
        tri[pl.ds(base, part), :] = total
        n2 = SIZE[axes[1]]
        part2 = part // n2
        s = fresh(n2 - 1)
        step2.append(launch([(
            tri.at[pl.ds(aligned(base + ((me[axes[1]] + d) % n2) * part2), part2)],
            buf2.at[c, pl.ds((n2 - 1 - d) * part2, part2)], peer(axes[1], d), s + n2 - 1 - d)
            for d in range(1, n2)]))
    for c, (axes, rows) in enumerate(COLOURS):
        for desc in step2[c]:
            desc.wait_recv()
        part = rows // SIZE[axes[0]]
        n2 = SIZE[axes[1]]
        part2 = part // n2
        base = aligned(mine + BASES[c] + me[axes[0]] * part + me[axes[1]] * part2)
        total = tri[pl.ds(base, part2), :]
        for k in range(n2 - 1):
            total = total + buf2[c, k * part2:(k + 1) * part2, :]
        tri[pl.ds(base, part2), :] = total
        n3 = SIZE[axes[2]]
        s = fresh(n3 - 1)
        step3.append(launch([(
            tri.at[pl.ds(base, part2)], buf3.at[c, pl.ds((n3 - 1 - d) * part2, part2)],
            peer(axes[2], d), s + n3 - 1 - d) for d in range(1, n3)]))
    gather2, gather1, gather0 = [], [], []
    for c, (axes, rows) in enumerate(COLOURS):
        for desc in step3[c]:
            desc.wait_recv()
        n2, n3 = SIZE[axes[1]], SIZE[axes[2]]
        part = rows // SIZE[axes[0]]
        part2 = part // n2
        base = aligned(mine + BASES[c] + me[axes[0]] * part + me[axes[1]] * part2)
        total = tri[pl.ds(base, part2), :]
        for k in range(n3 - 1):
            total = total + buf3[c, k * part2:(k + 1) * part2, :]
        tot[pl.ds(base, part2), :] = total
        s = fresh(n2 - 1)
        gather2.append(launch([(
            tot.at[pl.ds(base, part2)], tot.at[pl.ds(base, part2)], peer(axes[1], d), s + n2 - 1 - d)
            for d in range(1, n2)]))
    for c, (axes, rows) in enumerate(COLOURS):
        for desc in gather2[c]:
            desc.wait_recv()
        n = SIZE[axes[0]]
        part = rows // n
        base = aligned(mine + BASES[c] + me[axes[0]] * part)
        s = fresh(n - 1)
        gather1.append(launch([(
            tot.at[pl.ds(base, part)], tot.at[pl.ds(base, part)], peer(axes[0], d), s + n - 1 - d)
            for d in range(1, n)]))
    for c, (axes, rows) in enumerate(COLOURS):
        for desc in gather1[c]:
            desc.wait_recv()
        base = aligned(mine + BASES[c])
        s = fresh(1)
        gather0.append(launch([(tot.at[pl.ds(base, rows)], tot.at[pl.ds(base, rows)], partner, s)]))

    def post(d, carry):
        to = (g + d) % NG
        pltpu.make_async_remote_copy(
            src_ref=disp.at[pl.ds(aligned(to * SLOT, SLOT), SLOT)],
            dst_ref=arr.at[pl.ds(aligned(g * SLOT, SLOT), SLOT)],
            send_sem=a2a_send.at[0], recv_sem=a2a_recv.at[0],
            device_id=(to, r), device_id_type=MESH).start()
        return carry

    lax.fori_loop(1, NG, post, 0)
    arr[pl.ds(aligned(g * SLOT, SLOT), SLOT), :] = disp[pl.ds(aligned(g * SLOT, SLOT), SLOT), :]

    for c in range(3):
        for desc in gather0[c]:
            desc.wait_recv()

    inv_n = 1.0 / ROW_TOTAL
    acc[...] = jnp.zeros_like(acc)
    eye = jnp.where(iota((BLK, BLK), 0) == iota((BLK, BLK), 1), COV_EPS, 0.0)
    for i in range(8):
        mean_i = jnp.broadcast_to(tot[SUMS + i:SUMS + i + 1, :] * inv_n, (BLK, BLK))
        avg8[:, i * BLK:(i + 1) * BLK] = mean_i[0:8, :]
        mean_col = mean_i.T
        row = block_row(i, i)
        cov = tot[row:row + BLK, :] * inv_n - mean_col * mean_i + eye
        lin[i * BLK:(i + 1) * BLK, i * BLK:(i + 1) * BLK] = cov
        acc[...] += cov * cov

        def centre(j, carry, i=i, mean_col=mean_col):
            at = pl.ds(aligned((i * 8 - (i * (i - 1)) // 2 + (j - i)) * BLK, BLK), BLK)
            mean_j = tot[pl.ds(SUMS + j, 1), :] * inv_n
            cov = tot[at, :] * inv_n - mean_col * mean_j
            lin[i * BLK:(i + 1) * BLK, pl.ds(aligned(j * BLK, BLK), BLK)] = cov
            acc[...] += 2.0 * (cov * cov)
            return carry

        if i < 7:
            lax.fori_loop(i + 1, 8, centre, 0)
    squares = jnp.sum(jnp.sum(acc[...], axis=1, keepdims=True), axis=0, keepdims=True)
    scale = inverse_sqrt(squares)
    for i in range(8):
        def place(j, carry, i=i):
            v = lin[i * BLK:(i + 1) * BLK, pl.ds(aligned(j * BLK, BLK), BLK)] * scale
            hi, lo = split(v)
            vt = v.T
            hi_t, lo_t = split(vt)
            there = pl.ds(aligned(j * BLK, BLK), BLK)
            nh[there, i * BLK:(i + 1) * BLK] = hi_t
            nl[there, i * BLK:(i + 1) * BLK] = lo_t
            nh[i * BLK:(i + 1) * BLK, there] = hi
            nl[i * BLK:(i + 1) * BLK, there] = lo
            return carry

        lax.fori_loop(i, 8, place, 0)

    def product(terms, finish):
        def row(i, carry):
            def cell(j, carry):
                ri = pl.ds(aligned(i * MB, MB), MB)
                cj = pl.ds(aligned(j * MB, MB), MB)
                v = None
                for a, b in terms:
                    p = nn(a[ri, :], b[:, cj])
                    v = p if v is None else v + p
                finish(v, i, j, ri, cj)
                return carry
            lax.fori_loop(i, NB, cell, 0)
            return carry
        lax.fori_loop(0, NB, row, 0)

    def put(ref, v, ri, cj):
        ref[cj, ri] = v.T.astype(BF16)
        ref[ri, cj] = v.astype(BF16)

    def put2(hi_ref, lo_ref, v, ri, cj, both=False):
        hi, lo = split(v)
        vt = v.T
        if both:
            hi_t, lo_t = split(vt)
            hi_ref[cj, ri] = hi_t
            lo_ref[cj, ri] = lo_t
        else:
            hi_ref[cj, ri] = vt.astype(BF16)
        hi_ref[ri, cj] = hi
        lo_ref[ri, cj] = lo

    def read(hi_ref, lo_ref, ri, cj):
        return hi_ref[ri, cj].astype(F32) + lo_ref[ri, cj].astype(F32)

    def step_w(v, i, j, ri, cj):
        put(wh, 0.25 * v - 1.5 * read(nh, nl, ri, cj), ri, cj)

    product([(nh, nh)], step_w)

    def step_m(v, i, j, ri, cj):
        put2(mh, ml, v + 2.25 * read(nh, nl, ri, cj), ri, cj)

    product([(nh, wh)], step_m)

    def square(m_hi, m_lo, keep_lo):
        def run(v, i, j, ri, cj):
            m = read(m_hi, m_lo, ri, cj)
            put(eh, 1.125 * m - 0.125 * v, ri, cj)
            if keep_lo:
                put2(ah, al, v, ri, cj, both=True)
            else:
                put(ah, v, ri, cj)
            lin[ri, cj] = 1.6875 * v - 2.4375 * m
        return run

    product([(mh, mh)], square(mh, ml, False))

    def step_q(v, i, j, ri, cj):
        put2(qh, ql, lin[ri, cj] - 0.5 * v, ri, cj)

    product([(ah, eh)], step_q)

    def step_z(v, i, j, ri, cj):
        put2(zh, zl, 1.5 * read(qh, ql, ri, cj) - 1.125 * read(nh, nl, ri, cj) - 0.5 * v, ri, cj)

    product([(nh, qh)], step_z)

    def step_t(v, i, j, ri, cj):
        put2(th, tl, 2.25 * read(mh, ml, ri, cj) + v, ri, cj)

    product([(mh, qh)], step_t)

    def step_k(v, i, j, ri, cj):
        put2(kh, kl, 2.25 * read(th, tl, ri, cj) + v, ri, cj, both=True)

    product([(th, qh)], step_k)
    product([(kh, kh), (kh, kl), (kl, kh)], square(kh, kl, True))

    def step_q3(v, i, j, ri, cj):
        q = lin[ri, cj] - 0.5 * v
        put(qh, q, ri, cj)
        diag = jnp.where(iota((MB, MB), 0) + i * MB == iota((MB, MB), 1) + j * MB, 3.375 * 2.25, 0.0)
        lin[ri, cj] = 3.375 * q + diag + 2.25 * read(zh, zl, ri, cj)

    product([(ah, eh), (al, eh)], step_q3)

    def step_root(v, i, j, ri, cj):
        put(wh, lin[ri, cj] + v, ri, cj)

    product([(zh, qh)], step_root)

    sub = iota((8, D), 0)
    a0, a1, a2 = thirds(avg8[...])
    mean8 = jnp.where(sub == 0, a0.astype(F32),
                      jnp.where(sub == 1, a1.astype(F32), jnp.where(sub == 2, a2.astype(F32), 0.0)))
    off[...] = jnp.sum(nn(mean8.astype(BF16), wh[...]), axis=0, keepdims=True)

    pltpu.make_async_copy(arr.at[pl.ds(0, NROW - SLOT)], arr.at[pl.ds(0, NROW - SLOT)], a2a_recv.at[0]).wait()

    pick12 = jnp.where(iota((NG, NROW), 1) == iota((NG, NROW), 0) * SLOT + LABEL, 1.0, 0.0).astype(BF16)
    lab = nn(pick12, arr[:, 0:256]).astype(BF16)
    spread = jnp.where(iota((NROW, NG), 0) // SLOT == iota((NROW, NG), 1), 1.0, 0.0).astype(BF16)
    fold = jnp.where(iota((256, BLK), 0) % 16 == iota((256, BLK), 1), 1.0, 0.0).astype(BF16)
    full = nn(spread, lab)
    full = jnp.where(iota((NROW, 256), 1) // 16 == iota((NROW, 256), 0) % SLOT, full, 0.0).astype(BF16)
    member = nn(full, fold).astype(BF16)

    def whiten(i, carry):
        ri = pl.ds(aligned(i * MB, MB), MB)
        p = nn(arr[ri, :], wh[...]) - off[...]
        energy = jnp.sum(p * p, axis=1, keepdims=True)
        eh[ri, :] = (p * inverse_sqrt(energy + UNIT_EPS)).astype(BF16)
        return carry

    lax.fori_loop(0, NB, whiten, 0)
    ah[:, 0:BLK] = member

    def compare(i, carry):
        ri = pl.ds(aligned(i * MB, MB), MB)
        s = nt(eh[ri, :], eh[...])
        together = nt(ah[ri, 0:BLK], ah[:, 0:BLK])
        distinct = iota((MB, NROW), 0) + i * MB != iota((MB, NROW), 1)
        best = jnp.max(jnp.where((together > 0.5) & distinct, s, -1.0), axis=1, keepdims=True)
        best = jnp.maximum(best, -1.0)
        spot = iota((MB, BLK), 1) == iota((MB, BLK), 0) % SLOT
        lanes = jnp.where(spot, jnp.broadcast_to(best, (MB, BLK)), 0.0)
        ret[pl.ds(i * (MB // SLOT), MB // SLOT)] = jnp.sum(
            lanes.reshape(MB // SLOT, SLOT, BLK), axis=1, keepdims=True)
        return carry

    lax.fori_loop(0, NB, compare, 0)

    def answer(d, carry):
        to = (g + d) % NG
        pltpu.make_async_remote_copy(
            src_ref=ret.at[to], dst_ref=got.at[g], send_sem=a2a_send.at[1], recv_sem=a2a_recv.at[1],
            device_id=(to, r), device_id_type=MESH).start()
        return carry

    lax.fori_loop(1, NG, answer, 0)
    got[g] = ret[g]
    pltpu.make_async_copy(got.at[pl.ds(0, NG - 1)], got.at[pl.ds(0, NG - 1)], a2a_recv.at[1]).wait()

    rows = got[...].reshape(NG, BLK)
    owner_pick = jnp.where(iota((NG, ROWS), 0).astype(F32) == own_row, 1.0, 0.0).astype(BF16)
    picked = jnp.zeros((BLK, ROWS), F32)
    for part in thirds(rows.T):
        picked = picked + nn(part, owner_pick)
    hit = iota((BLK, ROWS), 0).astype(F32) == slot_row
    out[...] = jnp.sum(jnp.where(hit, picked, 0.0), axis=0, keepdims=True)

    for desc in every:
        desc.wait_send()
    pltpu.make_async_copy(disp.at[pl.ds(0, NROW - SLOT)], disp.at[pl.ds(0, NROW - SLOT)], a2a_send.at[0]).wait()
    pltpu.make_async_copy(ret.at[pl.ds(0, NG - 1)], ret.at[pl.ds(0, NG - 1)], a2a_send.at[1]).wait()


def sem_count():
    n = 0
    for axes, _ in COLOURS:
        a, b, c = (SIZE[k] - 1 for k in axes)
        n += 2 + 2 * a + 2 * b + c
    return n


def local(embeddings, scales, cluster, cluster_rank):
    vm = lambda shape, dtype: pltpu.VMEM(shape, dtype)
    mat = lambda: pltpu.VMEM((D, D), BF16)
    part2 = [rows // SIZE[a[0]] // SIZE[a[1]] for a, rows in COLOURS]
    scratch = [
        vm((ROWS, D), BF16),
        vm((2 * HALF, BLK), F32),
        vm((2 * HALF, BLK), F32),
        vm((HALF, BLK), F32),
        vm((HALF, BLK), F32),
        vm((3, max((SIZE[a[1]] - 1) * p for (a, _), p in zip(COLOURS, part2)), BLK), F32),
        vm((3, max((SIZE[a[2]] - 1) * p for (a, _), p in zip(COLOURS, part2)), BLK), F32),
        vm((NROW, D), BF16),
        vm((NROW, D), BF16),
        vm((NG, 1, BLK), F32),
        vm((NG, 1, BLK), F32),
    ] + [mat() for _ in range(16)] + [
        vm((D, D), F32),
        vm((BLK, BLK), F32),
        vm((8, D), F32),
        vm((1, D), F32),
        pltpu.SemaphoreType.DMA((sem_count(),)),
        pltpu.SemaphoreType.DMA((sem_count(),)),
        pltpu.SemaphoreType.DMA((2,)),
        pltpu.SemaphoreType.DMA((2,)),
    ]
    vmem = pl.BlockSpec(memory_space=pltpu.VMEM)
    best = pl.pallas_call(
        kernel,
        out_shape=jax.ShapeDtypeStruct((1, ROWS), F32),
        in_specs=[vmem, vmem, vmem],
        out_specs=vmem,
        scratch_shapes=scratch,
        compiler_params=pltpu.CompilerParams(
            collective_id=0, has_side_effects=True, vmem_limit_bytes=67043328),
    )(embeddings, scales, cluster.reshape(1, ROWS))
    return best.reshape(ROWS)


def solution(mesh):
    placed = (
        P(("grp", "rep"), None),
        P(("grp", "rep"), None),
        P(("grp", "rep")),
        P(("grp", "rep")),
    )
    return jax.shard_map(
        local, mesh=mesh, in_specs=placed, out_specs=P(("grp", "rep")), check_vma=False
    )
```
